256 devices in a mesh: span: 64 (over y_hi, x, z), rows: 4 (over y_lo, core).
Axes of the slice: x: 4, y: 4 (y_hi: 2, y_lo: 2; y = y_hi * 2 + y_lo), z: 8, core: 2. Of those that a mesh axis runs over, the one named last changes fastest.
Arguments:
- pressure_source: float32 [256, 128, 1024], P('span', 'rows'), may hold values from -6 to 6
- geometry: float32 [64, 3, 128, 1024], P('span', None, 'rows'), may hold values from 0.1 to 1
- owner: int32 [1], replicated, may hold values from 0 to 63
Outputs:
- pressure: float32 [256, 128, 1024], P('span', 'rows')
The draws below stay inside these ranges and needn't reach their ends.
Inputs may be any that keep to these rules, and one draw needn't show every extreme that they name: owner is a span index.
All inputs are finite; a program needn't handle non-finite values.
Results may differ from the reference program's by a relative error of at most 0.00011.
Values sent between devices are 32-bit elements; how exact they have to be, the bound alone decides.
A program may use at most 64 MiB of HBM per device.

```python
import math
import jax
import jax.numpy as jnp
from jax import lax

NZ = 256
NC = 1024
SWEEPS = 2
STEPS = 8
NR = 128
N_SPAN = 64


def log_between(key, shape, low, high):
    return jnp.exp(jax.random.uniform(key, shape, jnp.float32, math.log(low), math.log(high)))


def draw_geometry(key, part):
    keys = jax.random.split(jax.random.fold_in(key, 17), 6)
    shape = (N_SPAN, NR, NC)
    west_base = log_between(keys[0], shape, 0.1, 0.2)
    north_base = log_between(keys[1], shape, 0.1, 0.2)
    volume = log_between(keys[2], shape, 0.5, 1.0)
    north_band = log_between(keys[3], shape, 0.6, 1.0)
    west_band = log_between(keys[4], shape, 0.1, 0.13)
    band_width = NC // 4
    band_start = jax.random.randint(keys[5], (N_SPAN, 1, 1), 0, NC - band_width + 1)
    columns = jnp.arange(NC, dtype=jnp.int32)[None, None, :]
    inside = (columns >= band_start) & (columns < band_start + band_width)
    west_face = jnp.where(inside, west_band, west_base)
    north_face = jnp.where(inside, north_band, north_base)
    return jnp.stack([west_face, north_face, volume], axis=1).astype(jnp.float32)


def block_levels(own_key, shape, pieces, smallest, high):
    factor_of, own = 1.0, jax.random.fold_in(own_key, 6)
    for axis_at, blocks in pieces:
        steps = jnp.exp(jax.random.uniform(jax.random.fold_in(own, axis_at), (blocks,), jnp.float32, smallest / len(pieces), high / len(pieces)))
        factor_of = factor_of * jnp.repeat(steps, shape[axis_at] // blocks).reshape([-1 if axis == axis_at else 1 for axis in range(len(shape))])
    return factor_of


def gaussian(own_key, extent, spread, reach, cuts=(), kind=jnp.bfloat16):
    array = jax.random.normal(own_key, extent, jnp.float32) * spread
    if len(cuts) > 0:
        array = block_levels(own_key, extent, cuts, -0.22, 0.18) * array
    return jnp.clip(array, min=-reach, max=reach).astype(kind)


def setup_inputs(seed: int = 0) -> dict:
    seeds = jax.random.split(jax.random.key(seed), 4)
    return {
        "pressure_source": gaussian(seeds[0], (NZ, NR, NC), 1.0, 6.0, ((0, 64), (1, 4)), jnp.float32),
        "geometry": draw_geometry(jax.random.fold_in(seeds[3], 71), 0),
        "owner": jax.random.randint(seeds[2], (1,), 0, N_SPAN).astype(jnp.int32),
    }


LOWER_BOUND = 0.02
UPPER_BOUND = 2.0


def plane_operator(planes, coeffs):
    left_face, right_face, top_face, bottom_face, diagonal = coeffs
    zero_row = jnp.zeros_like(planes[:, :1])
    upper_rows = jnp.concatenate([zero_row, planes[:, :-1]], axis=1)
    lower_rows = jnp.concatenate([planes[:, 1:], zero_row], axis=1)
    zero_col = jnp.zeros_like(planes[:, :, :1])
    left_cols = jnp.concatenate([zero_col, planes[:, :, :-1]], axis=2)
    right_cols = jnp.concatenate([planes[:, :, 1:], zero_col], axis=2)
    return diagonal * planes - left_face * left_cols - right_face * right_cols - top_face * upper_rows - bottom_face * lower_rows


def chebyshev(rhs, coeffs):
    center = (UPPER_BOUND + LOWER_BOUND) / 2.0
    half_width = (UPPER_BOUND - LOWER_BOUND) / 2.0
    sigma_ratio = center / half_width
    inverse_diag = 1.0 / coeffs[4]
    solution = jnp.zeros_like(rhs)
    residual = rhs
    for sweep_index in range(SWEEPS):
        ratio_now = 1.0 / sigma_ratio
        direction = residual * inverse_diag / center
        for step_index in range(STEPS):
            solution = solution + direction
            residual = residual - plane_operator(direction, coeffs)
            ratio_next = 1.0 / (2.0 * sigma_ratio - ratio_now)
            direction = ratio_next * ratio_now * direction + (2.0 * ratio_next / half_width) * residual * inverse_diag
            ratio_now = ratio_next
    return solution


def reference(pressure_source, geometry, owner):
    plane = lax.dynamic_index_in_dim(geometry, owner[0], 0, keepdims=False)
    west_face = plane[0]
    north_face = plane[1]
    volume = plane[2]
    east_face = jnp.concatenate([west_face[:, 1:], jnp.zeros_like(west_face[:, :1])], axis=1)
    south_face = jnp.concatenate([north_face[1:], jnp.zeros_like(north_face[:1])], axis=0)
    face_total = west_face + east_face + north_face + south_face
    spectrum = jnp.fft.fft(pressure_source, axis=0)
    real_part = jnp.real(spectrum).astype(pressure_source.dtype)
    imag_part = jnp.imag(spectrum).astype(pressure_source.dtype)
    modes = jnp.arange(NZ, dtype=jnp.int32).astype(jnp.float32)
    eigen = 2.0 - 2.0 * jnp.cos(modes * (2.0 * jnp.pi / NZ))
    block_size = 8
    shape_rest = pressure_source.shape[1:]
    real_blocks = real_part.reshape((NZ // block_size, block_size) + shape_rest)
    imag_blocks = imag_part.reshape((NZ // block_size, block_size) + shape_rest)
    eigen_blocks = eigen.reshape((NZ // block_size, block_size))

    def solve_block(packed):
        real_block, imag_block, eigen_block = packed
        rhs = jnp.concatenate([real_block, imag_block], axis=0)
        eigen_both = jnp.concatenate([eigen_block, eigen_block], axis=0)
        diagonal = face_total[None] + eigen_both[:, None, None] * volume[None]
        coeffs = (west_face, east_face, north_face, south_face, diagonal)
        solved = chebyshev(rhs, coeffs)
        return solved[:block_size], solved[block_size:]

    solved_real, solved_imag = lax.map(solve_block, (real_blocks, imag_blocks, eigen_blocks))
    solved_real = solved_real.reshape((NZ,) + shape_rest)
    solved_imag = solved_imag.reshape((NZ,) + shape_rest)
    result = jnp.fft.ifft(lax.complex(solved_real, solved_imag), axis=0)
    return jnp.real(result).astype(pressure_source.dtype)
```

```python
import math

import jax
import jax.numpy as jnp
import ml_dtypes
import numpy as np
from jax import lax
from jax.experimental import pallas as pl
from jax.experimental.pallas import tpu as pltpu
from jax.sharding import PartitionSpec as P

MESH = pl.DeviceIdType.MESH
F32 = jnp.float32
BF16 = jnp.bfloat16

SWEEPS = 2
STEPS = 8
LOWER_BOUND = 0.02
UPPER_BOUND = 2.0
CENTER = (UPPER_BOUND + LOWER_BOUND) / 2.0
HALF_WIDTH = (UPPER_BOUND - LOWER_BOUND) / 2.0

NZ = 256
SPAN = 64
ROWS = 4
CELL_ROWS = NZ * 4
LANES = 128


def mode_numbers():
    slot = np.arange(NZ)
    return np.where(slot <= NZ // 2, slot, slot - NZ // 2), slot <= NZ // 2


def transform_tables():
    modes, is_real = mode_numbers()
    points = np.arange(NZ)
    angle = 2.0 * np.pi * ((modes[:, None] * points[None, :]) % NZ) / NZ
    forward = np.where(is_real[:, None], np.cos(angle), -np.sin(angle))
    weight = np.where((modes == 0) | (modes == NZ // 2), 1.0, 2.0)
    inverse = (forward * weight[:, None] / NZ).T
    pieces = []
    for table in (forward, inverse):
        high = table.astype(ml_dtypes.bfloat16)
        low = (table - high.astype(np.float64)).astype(ml_dtypes.bfloat16)
        pieces += [high, low]
    return np.stack(pieces)


def eigen_table():
    modes, _ = mode_numbers()
    return (2.0 - 2.0 * np.cos(2.0 * np.pi * modes / NZ)).astype(np.float32)


def step_table():
    sigma = CENTER / HALF_WIDTH
    keep, add = [], []
    for _ in range(SWEEPS):
        ratio = 1.0 / sigma
        for _ in range(STEPS):
            ratio_next = 1.0 / (2.0 * sigma - ratio)
            keep.append(ratio_next * ratio)
            add.append(2.0 * ratio_next / HALF_WIDTH)
            ratio = ratio_next
        keep[-1], add[-1] = 0.0, 1.0 / CENTER
    return np.array([keep, add], np.float32)


def transform(high, low, x):
    x_high = x.astype(BF16)
    x_low = (x - x_high.astype(F32)).astype(BF16)
    out = jnp.dot(high, x_high, preferred_element_type=F32)
    out += jnp.dot(high, x_low, preferred_element_type=F32)
    out += jnp.dot(low, x_high, preferred_element_type=F32)
    return out


def gathered(ref):
    return jnp.concatenate([ref[pl.ds(q, NZ, stride=4), :] for q in range(4)], axis=1)


def scattered(ref, value):
    for q in range(4):
        ref[pl.ds(q, NZ, stride=4), :] = value[:, q * LANES : (q + 1) * LANES]


def kernel(
    x_ref,
    g_ref,
    owner_ref,
    eigen_ref,
    step_ref,
    table_ref,
    o_ref,
    cells_out,
    cells_in,
    modes_out,
    plane_in,
    plane_out,
    modes_in,
    points_out,
    points_in,
    masked,
    part_x,
    sum_x,
    part_y,
    sum_y,
    part_z,
    geo,
    coef,
    zed,
    acc,
    ways,
    send_sem,
    recv_sem,
    geo_send,
    geo_recv,
    self_sem,
):
    span = lax.axis_index("span")
    row = lax.axis_index("rows")
    zi = lax.rem(span, 8)
    xi = lax.rem(lax.div(span, 8), 4)
    yh = lax.div(span, 32)
    yl = lax.div(row, 2)
    core = lax.rem(row, 2)
    mine = span * 4 + row
    place = 64 * row + span

    def span_peer(d):
        dz, dx, dy = lax.rem(d, 8), lax.rem(lax.div(d, 8), 4), lax.div(d, 32)
        return lax.rem(yh + dy, 2) * 32 + lax.rem(xi + dx, 4) * 8 + lax.rem(zi + dz, 8)

    def any_peer(d):
        dc, dl = lax.rem(d, 2), lax.rem(lax.div(d, 2), 2)
        return span_peer(lax.div(d, 4)), lax.rem(yl + dl, 2) * 2 + lax.rem(core + dc, 2)

    def rows_of(ref, start, size, unit):
        return ref.at[pl.ds(pl.multiple_of(start, unit), size)]

    def push(src, dst, sems, peer):
        pltpu.make_async_remote_copy(
            src_ref=src,
            dst_ref=dst,
            send_sem=sems[0],
            recv_sem=sems[1],
            device_id=peer,
            device_id_type=MESH,
        ).start()

    def await_rows(ref, count, sem):
        pltpu.make_async_copy(ref.at[pl.ds(0, count)], ref.at[pl.ds(0, count)], sem).wait()

    barrier = pltpu.get_barrier_semaphore()

    @pl.loop(1, SPAN)
    def _(d):
        pl.semaphore_signal(barrier, inc=1, device_id=(span_peer(d), row), device_id_type=MESH)

    for d in range(1, ROWS):
        pl.semaphore_signal(
            barrier, inc=1, device_id=(span, lax.rem(row + d, ROWS)), device_id_type=MESH
        )

    own = owner_ref[0] == span
    for x_to in range(4):
        for y_to in range(2):
            tile_row, half = divmod(y_to * 4 + x_to, 2)
            for z_to in range(8):
                for comp in range(3):
                    piece = g_ref[comp, 8 * tile_row + 4 * half : 8 * tile_row + 4 * half + 4,
                                  z_to * LANES : (z_to + 1) * LANES]
                    at = ((x_to * 2 + y_to) * 8 + z_to) * 12 + comp * 4
                    masked[at : at + 4, :] = jnp.where(own, piece, jnp.zeros_like(piece))

    for to in range(SPAN):
        rows_at, cols_at = 4 * (to // 8), LANES * (to % 8)
        for j in range(4):
            cells_out[16 * to + 4 * j : 16 * to + 4 * j + 4, :] = x_ref[
                j, rows_at : rows_at + 4, cols_at : cols_at + LANES
            ]

    pl.semaphore_wait(barrier, SPAN - 1 + ROWS - 1)

    def geo_sems(k):
        return geo_send.at[k], geo_recv.at[k]

    def span_at(y, x, z):
        return y * 32 + x * 8 + z

    for d in range(1, 4):
        to = lax.rem(xi + d, 4)
        push(
            rows_of(masked, to * 192, 192, 8),
            rows_of(part_x, xi * 192, 192, 8),
            geo_sems(0),
            (span_at(yh, to, zi), row),
        )

    def sems(k):
        return send_sem.at[k], recv_sem.at[k]

    @pl.loop(1, SPAN)
    def _(d):
        to = span_peer(d)
        push(
            rows_of(cells_out, to * 16, 16, 16),
            rows_of(cells_in, span * 16, 16, 16),
            sems(0),
            (to, row),
        )

    cells_in[pl.ds(pl.multiple_of(span * 16, 16), 16), :] = cells_out[
        pl.ds(pl.multiple_of(span * 16, 16), 16), :
    ]
    part_x[pl.ds(pl.multiple_of(xi * 192, 8), 192), :] = masked[
        pl.ds(pl.multiple_of(xi * 192, 8), 192), :
    ]

    await_rows(part_x, 576, geo_recv.at[0])
    sum_x[...] = part_x[0:192] + part_x[192:384] + part_x[384:576] + part_x[576:768]
    push(
        rows_of(sum_x, (1 - yh) * 96, 96, 8),
        part_y,
        geo_sems(1),
        (span_at(1 - yh, xi, zi), row),
    )
    await_rows(part_y, 96, geo_recv.at[1])
    sum_y[...] = part_y[...] + sum_x[pl.ds(pl.multiple_of(yh * 96, 8), 96), :]
    for d in range(1, 8):
        to = lax.rem(zi + d, 8)
        push(
            rows_of(sum_y, to * 12, 12, 4),
            rows_of(part_z, zi * 16, 12, 4),
            geo_sems(2),
            (span_at(yh, xi, to), row),
        )
    keep_z = pltpu.make_async_copy(
        rows_of(sum_y, zi * 12, 12, 4), rows_of(part_z, zi * 16, 12, 4), self_sem.at[0]
    )
    keep_z.start()
    keep_z.wait()
    await_rows(part_z, 84, geo_recv.at[2])
    total = part_z[0:12]
    for d in range(1, 8):
        total = total + part_z[16 * d : 16 * d + 12]
    sum_y_own = masked.at[pl.ds(768, 12)]
    masked[768:780, :] = total

    here = 12 * place
    for d in range(1, 8):
        push(
            sum_y_own,
            rows_of(geo, here, 12, 4),
            geo_sems(3),
            (span_at(yh, xi, lax.rem(zi + d, 8)), row),
        )
    keep_geo = pltpu.make_async_copy(sum_y_own, rows_of(geo, here, 12, 4), self_sem.at[1])
    keep_geo.start()
    keep_geo.wait()

    await_rows(cells_in, 1008, recv_sem.at[0])
    scattered(modes_out, transform(table_ref[0], table_ref[1], gathered(cells_in)))

    @pl.loop(1, NZ)
    def _(d):
        to_span, to_row = any_peer(d)
        push(
            rows_of(modes_out, (to_span * 4 + to_row) * 4, 4, 4),
            rows_of(plane_in, place * 4, 4, 4),
            sems(1),
            (to_span, to_row),
        )

    keep_plane = pltpu.make_async_copy(
        rows_of(modes_out, mine * 4, 4, 4), rows_of(plane_in, place * 4, 4, 4), self_sem.at[2]
    )
    keep_plane.start()
    keep_plane.wait()

    def block(r, y, x):
        return rows_of(geo, 12 * (64 * r + 32 * y + 8 * x), 96, 8)

    await_rows(geo, 84, geo_recv.at[3])
    for d in range(1, 4):
        y_to, l_to = lax.rem(yh + d // 2, 2), lax.rem(yl + d % 2, 2)
        push(
            block(row, yh, xi),
            block(row, yh, xi),
            geo_sems(4),
            (span_at(y_to, xi, zi), 2 * l_to + core),
        )
    await_rows(geo, 288, geo_recv.at[4])
    for d in range(1, 4):
        to = lax.rem(xi + d, 4)
        for l in range(2):
            for y in range(2):
                push(
                    block(2 * l + core, y, xi),
                    block(2 * l + core, y, xi),
                    geo_sems(5),
                    (span_at(yh, to, zi), row),
                )
    await_rows(geo, 1152, geo_recv.at[5])
    for l in range(2):
        push(
            rows_of(geo, 768 * (2 * l + core), 768, 8),
            rows_of(geo, 768 * (2 * l + core), 768, 8),
            geo_sems(6),
            (span, 2 * yl + 1 - core),
        )
    await_rows(geo, 1536, geo_recv.at[6])

    await_rows(plane_in, 1020, recv_sem.at[1])

    eigen = eigen_ref[mine]
    lane = lax.broadcasted_iota(jnp.int32, (8, LANES), 1)
    sub = lax.broadcasted_iota(jnp.int32, (8, LANES), 0)
    first_lane, last_lane = lane == 0, lane == LANES - 1
    first_sub, last_sub = sub == 0, sub == 7

    def face(comp, x, q, z):
        return geo[pl.ds(12 * (8 * x + z) + 4 * comp + q, 8, stride=384), :]

    def slot(i, z):
        return pl.ds(pl.multiple_of((i * 8 + z) * 8, 8), 8)

    def way(parity, i, z):
        return pl.ds(pl.multiple_of(parity * 1152 + ((i + 1) * 8 + z) * 8, 8), 8)

    def to_left(v):
        return pltpu.roll(v, LANES - 1, 1)

    def to_right(v):
        return pltpu.roll(v, 1, 1)

    for x in range(4):
        for q in range(4):
            i = 4 * x + q
            west = [face(0, x, q, z) for z in range(8)]
            moved = [to_left(w) for w in west] + [jnp.zeros((8, LANES), F32)]
            for z in range(8):
                north = face(1, x, q, z)
                if i < 15:
                    south = face(1, (i + 1) // 4, (i + 1) % 4, z)
                else:
                    south = jnp.where(last_sub, 0.0, pltpu.roll(face(1, 0, 0, z), 7, 0))
                east = jnp.where(last_lane, moved[z + 1], moved[z])
                inverse = 1.0 / (west[z] + east + north + south + eigen * face(2, x, q, z))
                west_in = jnp.where(first_lane, 0.0, west[z]) if z == 0 else west[z]
                north_in = jnp.where(first_sub, 0.0, north) if i == 0 else north
                coef[0, slot(i, z), :] = west_in * inverse
                coef[1, slot(i, z), :] = east * inverse
                coef[2, slot(i, z), :] = north_in * inverse
                coef[3, slot(i, z), :] = south * inverse
                value = plane_in[pl.ds(4 * (8 * x + z) + q, 8, stride=128), :] * inverse
                zed[slot(i, z), :] = value
                way_0 = value * (1.0 / CENTER)
                ways[way(0, i, z), :] = way_0
                acc[slot(i, z), :] = jnp.zeros((8, LANES), F32)
                if i == 15:
                    ways[way(0, -1, z), :] = pltpu.roll(way_0, 1, 0)
                if i == 0:
                    ways[way(0, 16, z), :] = pltpu.roll(way_0, 7, 0)

    def one_step(step, carry):
        now = lax.rem(step, 2)
        later = 1 - now
        keep, add = step_ref[0, step], step_ref[1, step]

        def one_row(i, carry):
            mid = [ways[way(now, i, z), :] for z in range(8)]
            right = [to_right(m) for m in mid]
            left = [to_left(m) for m in mid]
            for z in range(8):
                from_west = jnp.where(first_lane, right[z - 1], right[z]) if z else right[z]
                from_east = jnp.where(last_lane, left[z + 1], left[z]) if z < 7 else left[z]
                flow = coef[0, slot(i, z), :] * from_west + coef[1, slot(i, z), :] * from_east
                flow += coef[2, slot(i, z), :] * ways[way(now, i - 1, z), :]
                flow += coef[3, slot(i, z), :] * ways[way(now, i + 1, z), :]
                value = zed[slot(i, z), :] - mid[z] + flow
                zed[slot(i, z), :] = value
                acc[slot(i, z), :] += mid[z]
                ways[way(later, i, z), :] = keep * mid[z] + add * value
            return carry

        lax.fori_loop(0, 16, one_row, 0)
        for z in range(8):
            ways[way(later, -1, z), :] = pltpu.roll(ways[way(later, 15, z), :], 1, 0)
            ways[way(later, 16, z), :] = pltpu.roll(ways[way(later, 0, z), :], 7, 0)
        return carry

    last = SWEEPS * STEPS - 1
    lax.fori_loop(0, last, one_step, 0)
    for x in range(4):
        for q in range(4):
            i = 4 * x + q
            for z in range(8):
                plane_out[pl.ds(4 * (8 * x + z) + q, 8, stride=128), :] = (
                    acc[slot(i, z), :] + ways[way(last % 2, i, z), :]
                )

    @pl.loop(1, NZ)
    def _(d):
        to_span, to_row = any_peer(d)
        push(
            rows_of(plane_out, (64 * to_row + to_span) * 4, 4, 4),
            rows_of(modes_in, mine * 4, 4, 4),
            sems(2),
            (to_span, to_row),
        )

    keep_modes = pltpu.make_async_copy(
        rows_of(plane_out, place * 4, 4, 4), rows_of(modes_in, mine * 4, 4, 4), self_sem.at[3]
    )
    keep_modes.start()
    keep_modes.wait()
    await_rows(modes_in, 1020, recv_sem.at[2])
    scattered(points_out, transform(table_ref[2], table_ref[3], gathered(modes_in)))

    @pl.loop(1, SPAN)
    def _(d):
        to = span_peer(d)
        push(
            rows_of(points_out, to * 16, 16, 16),
            rows_of(points_in, span * 16, 16, 16),
            sems(3),
            (to, row),
        )

    points_in[pl.ds(pl.multiple_of(span * 16, 16), 16), :] = points_out[
        pl.ds(pl.multiple_of(span * 16, 16), 16), :
    ]
    await_rows(points_in, 1008, recv_sem.at[3])
    for source in range(SPAN):
        rows_at, cols_at = 4 * (source // 8), LANES * (source % 8)
        for j in range(4):
            o_ref[j, rows_at : rows_at + 4, cols_at : cols_at + LANES] = points_in[
                16 * source + 4 * j : 16 * source + 4 * j + 4, :
            ]

    await_rows(cells_out, 1008, send_sem.at[0])
    await_rows(modes_out, 1020, send_sem.at[1])
    await_rows(plane_out, 1020, send_sem.at[2])
    await_rows(points_out, 1008, send_sem.at[3])
    for k, count in enumerate((576, 96, 84, 84, 288, 1152, 1536)):
        await_rows(geo, count, geo_send.at[k])


def on_device(pressure_source, geometry, owner, eigen, steps, tables):
    vmem = pl.BlockSpec(memory_space=pltpu.VMEM)
    smem = pl.BlockSpec(memory_space=pltpu.SMEM)
    cells = pltpu.VMEM((CELL_ROWS, LANES), F32)
    return pl.pallas_call(
        kernel,
        out_shape=jax.ShapeDtypeStruct(pressure_source.shape, F32),
        in_specs=[vmem, vmem, smem, smem, smem, vmem],
        out_specs=vmem,
        scratch_shapes=[cells] * 8
        + [
            pltpu.VMEM((784, LANES), F32),
            pltpu.VMEM((768, LANES), F32),
            pltpu.VMEM((192, LANES), F32),
            pltpu.VMEM((96, LANES), F32),
            pltpu.VMEM((96, LANES), F32),
            pltpu.VMEM((128, LANES), F32),
            pltpu.VMEM((3072, LANES), F32),
            pltpu.VMEM((4, CELL_ROWS, LANES), F32),
            cells,
            cells,
            pltpu.VMEM((2304, LANES), F32),
            pltpu.SemaphoreType.DMA((4,)),
            pltpu.SemaphoreType.DMA((4,)),
            pltpu.SemaphoreType.DMA((7,)),
            pltpu.SemaphoreType.DMA((7,)),
            pltpu.SemaphoreType.DMA((4,)),
        ],
        compiler_params=pltpu.CompilerParams(
            collective_id=0, has_side_effects=True, vmem_limit_bytes=48 * 2**20
        ),
    )(pressure_source, geometry[0], owner, eigen, steps, tables)


def solution(mesh):
    eigen, steps, tables = eigen_table(), step_table(), transform_tables()

    def whole(pressure_source, geometry, owner):
        return jax.shard_map(
            on_device,
            mesh=mesh,
            in_specs=(P("span", "rows", None), P("span", None, "rows", None), P(), P(), P(), P()),
            out_specs=P("span", "rows", None),
            check_vma=False,
        )(pressure_source, geometry, owner, eigen, steps, tables)

    return whole
```

```python
import math

import jax
import jax.numpy as jnp
import ml_dtypes
import numpy as np
from jax import lax
from jax.experimental import pallas as pl
from jax.experimental.pallas import tpu as pltpu
from jax.sharding import PartitionSpec as P

MESH = pl.DeviceIdType.MESH
F32 = jnp.float32
BF16 = jnp.bfloat16

SWEEPS = 2
STEPS = 8
LOWER_BOUND = 0.02
UPPER_BOUND = 2.0
CENTER = (UPPER_BOUND + LOWER_BOUND) / 2.0
HALF_WIDTH = (UPPER_BOUND - LOWER_BOUND) / 2.0

NZ = 256
SPAN = 64
ROWS = 4
CELL_ROWS = NZ * 4
LANES = 128


def mode_numbers():
    slot = np.arange(NZ)
    return np.where(slot <= NZ // 2, slot, slot - NZ // 2), slot <= NZ // 2


def transform_tables():
    modes, is_real = mode_numbers()
    points = np.arange(NZ)
    angle = 2.0 * np.pi * ((modes[:, None] * points[None, :]) % NZ) / NZ
    forward = np.where(is_real[:, None], np.cos(angle), -np.sin(angle))
    weight = np.where((modes == 0) | (modes == NZ // 2), 1.0, 2.0)
    inverse = (forward * weight[:, None] / NZ).T
    pieces = []
    for table in (forward, inverse):
        high = table.astype(ml_dtypes.bfloat16)
        low = (table - high.astype(np.float64)).astype(ml_dtypes.bfloat16)
        pieces += [high, low]
    return np.stack(pieces)


def eigen_table():
    modes, _ = mode_numbers()
    return (2.0 - 2.0 * np.cos(2.0 * np.pi * modes / NZ)).astype(np.float32)


def step_table():
    sigma = CENTER / HALF_WIDTH
    keep, add = [], []
    for _ in range(SWEEPS):
        ratio = 1.0 / sigma
        for _ in range(STEPS):
            ratio_next = 1.0 / (2.0 * sigma - ratio)
            keep.append(ratio_next * ratio)
            add.append(2.0 * ratio_next / HALF_WIDTH)
            ratio = ratio_next
        keep[-1], add[-1] = 0.0, 1.0 / CENTER
    return np.array([keep, add], np.float32)


def transform(high, low, x):
    x_high = x.astype(BF16)
    x_low = (x - x_high.astype(F32)).astype(BF16)
    out = jnp.dot(high, x_high, preferred_element_type=F32)
    out += jnp.dot(high, x_low, preferred_element_type=F32)
    out += jnp.dot(low, x_high, preferred_element_type=F32)
    return out


def gathered(ref):
    return jnp.concatenate([ref[pl.ds(q, NZ, stride=4), :] for q in range(4)], axis=1)


def scattered(ref, value):
    for q in range(4):
        ref[pl.ds(q, NZ, stride=4), :] = value[:, q * LANES : (q + 1) * LANES]


def kernel(
    x_hbm,
    g_hbm,
    owner_ref,
    eigen_ref,
    step_ref,
    table_hbm,
    o_ref,
    x_ref,
    g_ref,
    table_ref,
    cells_out,
    cells_in,
    modes_out,
    plane_in,
    plane_out,
    modes_in,
    points_out,
    points_in,
    masked,
    part_x,
    sum_x,
    part_y,
    sum_y,
    part_z,
    geo,
    coef,
    zed,
    acc,
    way_a,
    way_b,
    in_sem,
    send_sem,
    recv_sem,
    geo_send,
    geo_recv,
    self_sem,
):
    span = lax.axis_index("span")
    row = lax.axis_index("rows")
    zi = lax.rem(span, 8)
    xi = lax.rem(lax.div(span, 8), 4)
    yh = lax.div(span, 32)
    yl = lax.div(row, 2)
    core = lax.rem(row, 2)
    mine = span * 4 + row
    place = 64 * row + span

    def span_peer(d):
        dz, dx, dy = lax.rem(d, 8), lax.rem(lax.div(d, 8), 4), lax.div(d, 32)
        return lax.rem(yh + dy, 2) * 32 + lax.rem(xi + dx, 4) * 8 + lax.rem(zi + dz, 8)

    def any_peer(d):
        dc, dl = lax.rem(d, 2), lax.rem(lax.div(d, 2), 2)
        return span_peer(lax.div(d, 4)), lax.rem(yl + dl, 2) * 2 + lax.rem(core + dc, 2)

    def rows_of(ref, start, size, unit):
        return ref.at[pl.ds(pl.multiple_of(start, unit), size)]

    def push(src, dst, sems, peer):
        pltpu.make_async_remote_copy(
            src_ref=src,
            dst_ref=dst,
            send_sem=sems[0],
            recv_sem=sems[1],
            device_id=peer,
            device_id_type=MESH,
        ).start()

    def await_rows(ref, count, sem):
        pltpu.make_async_copy(ref.at[pl.ds(0, count)], ref.at[pl.ds(0, count)], sem).wait()

    fetch = [
        pltpu.make_async_copy(src, dst, in_sem.at[k])
        for k, (src, dst) in enumerate(
            ((x_hbm, x_ref), (g_hbm, g_ref), (table_hbm, table_ref))
        )
    ]
    for copy in fetch:
        copy.start()

    barrier = pltpu.get_barrier_semaphore()

    @pl.loop(1, SPAN)
    def _(d):
        pl.semaphore_signal(barrier, inc=1, device_id=(span_peer(d), row), device_id_type=MESH)

    for d in range(1, ROWS):
        pl.semaphore_signal(
            barrier, inc=1, device_id=(span, lax.rem(row + d, ROWS)), device_id_type=MESH
        )

    fetch[1].wait()
    own = owner_ref[0] == span
    for x_to in range(4):
        for y_to in range(2):
            tile_row, half = divmod(y_to * 4 + x_to, 2)
            for z_to in range(8):
                for comp in range(3):
                    piece = g_ref[comp, 8 * tile_row + 4 * half : 8 * tile_row + 4 * half + 4,
                                  z_to * LANES : (z_to + 1) * LANES]
                    at = ((x_to * 2 + y_to) * 8 + z_to) * 12 + comp * 4
                    masked[at : at + 4, :] = jnp.where(own, piece, jnp.zeros_like(piece))

    fetch[0].wait()
    for to in range(SPAN):
        rows_at, cols_at = 4 * (to // 8), LANES * (to % 8)
        for j in range(4):
            cells_out[16 * to + 4 * j : 16 * to + 4 * j + 4, :] = x_ref[
                j, rows_at : rows_at + 4, cols_at : cols_at + LANES
            ]

    pl.semaphore_wait(barrier, SPAN - 1 + ROWS - 1)

    def geo_sems(k):
        return geo_send.at[k], geo_recv.at[k]

    def span_at(y, x, z):
        return y * 32 + x * 8 + z

    for d in range(1, 4):
        to = lax.rem(xi + d, 4)
        push(
            rows_of(masked, to * 192, 192, 8),
            rows_of(part_x, xi * 192, 192, 8),
            geo_sems(0),
            (span_at(yh, to, zi), row),
        )

    def sems(k):
        return send_sem.at[k], recv_sem.at[k]

    @pl.loop(1, SPAN)
    def _(d):
        to = span_peer(d)
        push(
            rows_of(cells_out, to * 16, 16, 16),
            rows_of(cells_in, span * 16, 16, 16),
            sems(0),
            (to, row),
        )

    cells_in[pl.ds(pl.multiple_of(span * 16, 16), 16), :] = cells_out[
        pl.ds(pl.multiple_of(span * 16, 16), 16), :
    ]
    part_x[pl.ds(pl.multiple_of(xi * 192, 8), 192), :] = masked[
        pl.ds(pl.multiple_of(xi * 192, 8), 192), :
    ]

    await_rows(part_x, 576, geo_recv.at[0])
    sum_x[...] = part_x[0:192] + part_x[192:384] + part_x[384:576] + part_x[576:768]
    push(
        rows_of(sum_x, (1 - yh) * 96, 96, 8),
        part_y,
        geo_sems(1),
        (span_at(1 - yh, xi, zi), row),
    )
    await_rows(part_y, 96, geo_recv.at[1])
    sum_y[...] = part_y[...] + sum_x[pl.ds(pl.multiple_of(yh * 96, 8), 96), :]
    for d in range(1, 8):
        to = lax.rem(zi + d, 8)
        push(
            rows_of(sum_y, to * 12, 12, 4),
            rows_of(part_z, zi * 16, 12, 4),
            geo_sems(2),
            (span_at(yh, xi, to), row),
        )
    keep_z = pltpu.make_async_copy(
        rows_of(sum_y, zi * 12, 12, 4), rows_of(part_z, zi * 16, 12, 4), self_sem.at[0]
    )
    keep_z.start()
    await_rows(part_z, 84, geo_recv.at[2])
    keep_z.wait()
    total = part_z[0:12]
    for d in range(1, 8):
        total = total + part_z[16 * d : 16 * d + 12]
    sum_y_own = masked.at[pl.ds(768, 12)]
    masked[768:780, :] = total

    here = 12 * place
    for d in range(1, 8):
        push(
            sum_y_own,
            rows_of(geo, here, 12, 4),
            geo_sems(3),
            (span_at(yh, xi, lax.rem(zi + d, 8)), row),
        )
    keep_geo = pltpu.make_async_copy(sum_y_own, rows_of(geo, here, 12, 4), self_sem.at[1])
    keep_geo.start()

    await_rows(cells_in, 1008, recv_sem.at[0])
    fetch[2].wait()
    scattered(modes_out, transform(table_ref[0], table_ref[1], gathered(cells_in)))

    @pl.loop(1, NZ)
    def _(d):
        to_span, to_row = any_peer(d)
        push(
            rows_of(modes_out, (to_span * 4 + to_row) * 4, 4, 4),
            rows_of(plane_in, place * 4, 4, 4),
            sems(1),
            (to_span, to_row),
        )

    keep_plane = pltpu.make_async_copy(
        rows_of(modes_out, mine * 4, 4, 4), rows_of(plane_in, place * 4, 4, 4), self_sem.at[2]
    )
    keep_plane.start()

    def block(r, y, x):
        return rows_of(geo, 12 * (64 * r + 32 * y + 8 * x), 96, 8)

    await_rows(geo, 84, geo_recv.at[3])
    keep_geo.wait()
    for d in range(1, 4):
        y_to, l_to = lax.rem(yh + d // 2, 2), lax.rem(yl + d % 2, 2)
        push(
            block(row, yh, xi),
            block(row, yh, xi),
            geo_sems(4),
            (span_at(y_to, xi, zi), 2 * l_to + core),
        )
    await_rows(geo, 288, geo_recv.at[4])
    for d in range(1, 4):
        to = lax.rem(xi + d, 4)
        for l in range(2):
            for y in range(2):
                push(
                    block(2 * l + core, y, xi),
                    block(2 * l + core, y, xi),
                    geo_sems(5),
                    (span_at(yh, to, zi), row),
                )
    await_rows(geo, 1152, geo_recv.at[5])
    for l in range(2):
        push(
            rows_of(geo, 768 * (2 * l + core), 768, 8),
            rows_of(geo, 768 * (2 * l + core), 768, 8),
            geo_sems(6),
            (span, 2 * yl + 1 - core),
        )
    await_rows(geo, 1536, geo_recv.at[6])

    await_rows(plane_in, 1020, recv_sem.at[1])
    keep_plane.wait()

    eigen = eigen_ref[mine]
    lane = lax.broadcasted_iota(jnp.int32, (8, LANES), 1)
    sub = lax.broadcasted_iota(jnp.int32, (8, LANES), 0)
    first_lane, last_lane = lane == 0, lane == LANES - 1
    first_sub, last_sub = sub == 0, sub == 7

    def face(comp, x, q, z):
        return geo[pl.ds(12 * (8 * x + z) + 4 * comp + q, 8, stride=384), :]

    def slot(i, z):
        return pl.ds((i * 8 + z) * 8, 8)

    def to_left(v):
        return pltpu.roll(v, LANES - 1, 1)

    def to_right(v):
        return pltpu.roll(v, 1, 1)

    for x in range(4):
        for q in range(4):
            i = 4 * x + q
            west = [face(0, x, q, z) for z in range(8)]
            moved = [to_left(w) for w in west] + [jnp.zeros((8, LANES), F32)]
            for z in range(8):
                north = face(1, x, q, z)
                if i < 15:
                    south = face(1, (i + 1) // 4, (i + 1) % 4, z)
                else:
                    south = jnp.where(last_sub, 0.0, pltpu.roll(face(1, 0, 0, z), 7, 0))
                east = jnp.where(last_lane, moved[z + 1], moved[z])
                inverse = 1.0 / (west[z] + east + north + south + eigen * face(2, x, q, z))
                west_in = jnp.where(first_lane, 0.0, west[z]) if z == 0 else west[z]
                north_in = jnp.where(first_sub, 0.0, north) if i == 0 else north
                coef[0, slot(i, z), :] = west_in * inverse
                coef[1, slot(i, z), :] = east * inverse
                coef[2, slot(i, z), :] = north_in * inverse
                coef[3, slot(i, z), :] = south * inverse
                value = plane_in[pl.ds(4 * (8 * x + z) + q, 8, stride=128), :] * inverse
                zed[slot(i, z), :] = value
                way_a[slot(i, z), :] = value * (1.0 / CENTER)
                acc[slot(i, z), :] = jnp.zeros((8, LANES), F32)

    lanes = lax.broadcasted_iota(jnp.int32, (64, LANES), 1)
    first_lanes, last_lanes = lanes == 0, lanes == LANES - 1

    def line(i):
        return pl.ds(64 * i, 64)

    def turned(v, shift):
        return jnp.concatenate(
            [pltpu.roll(v[8 * z : 8 * z + 8], shift, 0) for z in range(8)], axis=0
        )

    def residuals(ways, done):
        above, mid = turned(ways[line(15), :], 1), ways[line(0), :]
        for i in range(16):
            below = ways[line(i + 1), :] if i < 15 else turned(ways[line(0), :], 7)
            right, left = to_right(mid), to_left(mid)
            from_west = jnp.where(
                first_lanes, jnp.concatenate([right[56:], right[:56]], axis=0), right
            )
            from_east = jnp.where(
                last_lanes, jnp.concatenate([left[8:], left[:8]], axis=0), left
            )
            flow = coef[0, line(i), :] * from_west + coef[1, line(i), :] * from_east
            flow += coef[2, line(i), :] * above + coef[3, line(i), :] * below
            done(i, mid, zed[line(i), :] - mid + flow)
            above, mid = mid, below

    def two_steps(pair, carry):
        keep_a, add_a = step_ref[0, 2 * pair], step_ref[1, 2 * pair]
        keep_b, add_b = step_ref[0, 2 * pair + 1], step_ref[1, 2 * pair + 1]

        def first_done(i, mid, value):
            zed[line(i), :] = value
            way_b[line(i), :] = keep_a * mid + add_a * value

        def second_done(i, mid, value):
            zed[line(i), :] = value
            acc[line(i), :] += way_a[line(i), :] + mid
            way_a[line(i), :] = keep_b * mid + add_b * value

        residuals(way_a, first_done)
        residuals(way_b, second_done)
        return carry

    last = SWEEPS * STEPS - 2
    lax.fori_loop(0, last // 2, two_steps, 0)
    keep, add = step_ref[0, last], step_ref[1, last]

    def last_done(i, mid, value):
        total = acc[line(i), :] + mid + (keep * mid + add * value)
        x, q = divmod(i, 4)
        for z in range(8):
            plane_out[pl.ds(4 * (8 * x + z) + q, 8, stride=128), :] = total[8 * z : 8 * z + 8]

    residuals(way_a, last_done)

    @pl.loop(1, NZ)
    def _(d):
        to_span, to_row = any_peer(d)
        push(
            rows_of(plane_out, (64 * to_row + to_span) * 4, 4, 4),
            rows_of(modes_in, mine * 4, 4, 4),
            sems(2),
            (to_span, to_row),
        )

    keep_modes = pltpu.make_async_copy(
        rows_of(plane_out, place * 4, 4, 4), rows_of(modes_in, mine * 4, 4, 4), self_sem.at[3]
    )
    keep_modes.start()
    await_rows(modes_in, 1020, recv_sem.at[2])
    keep_modes.wait()
    scattered(points_out, transform(table_ref[2], table_ref[3], gathered(modes_in)))

    @pl.loop(1, SPAN)
    def _(d):
        to = span_peer(d)
        push(
            rows_of(points_out, to * 16, 16, 16),
            rows_of(points_in, span * 16, 16, 16),
            sems(3),
            (to, row),
        )

    points_in[pl.ds(pl.multiple_of(span * 16, 16), 16), :] = points_out[
        pl.ds(pl.multiple_of(span * 16, 16), 16), :
    ]
    await_rows(points_in, 1008, recv_sem.at[3])
    for source in range(SPAN):
        rows_at, cols_at = 4 * (source // 8), LANES * (source % 8)
        for j in range(4):
            o_ref[j, rows_at : rows_at + 4, cols_at : cols_at + LANES] = points_in[
                16 * source + 4 * j : 16 * source + 4 * j + 4, :
            ]

    await_rows(cells_out, 1008, send_sem.at[0])
    await_rows(modes_out, 1020, send_sem.at[1])
    await_rows(plane_out, 1020, send_sem.at[2])
    await_rows(points_out, 1008, send_sem.at[3])
    for k, count in enumerate((576, 96, 84, 84, 288, 1152, 1536)):
        await_rows(geo, count, geo_send.at[k])


def on_device(pressure_source, geometry, owner, eigen, steps, tables):
    vmem = pl.BlockSpec(memory_space=pltpu.VMEM)
    hbm = pl.BlockSpec(memory_space=pltpu.HBM)
    smem = pl.BlockSpec(memory_space=pltpu.SMEM)
    cells = pltpu.VMEM((CELL_ROWS, LANES), F32)
    return pl.pallas_call(
        kernel,
        out_shape=jax.ShapeDtypeStruct(pressure_source.shape, F32),
        in_specs=[hbm, hbm, smem, smem, smem, hbm],
        out_specs=vmem,
        scratch_shapes=[
            pltpu.VMEM(pressure_source.shape, F32),
            pltpu.VMEM(geometry.shape[1:], F32),
            pltpu.VMEM(tables.shape, BF16),
        ]
        + [cells] * 8
        + [
            pltpu.VMEM((784, LANES), F32),
            pltpu.VMEM((768, LANES), F32),
            pltpu.VMEM((192, LANES), F32),
            pltpu.VMEM((96, LANES), F32),
            pltpu.VMEM((96, LANES), F32),
            pltpu.VMEM((128, LANES), F32),
            pltpu.VMEM((3072, LANES), F32),
            pltpu.VMEM((4, CELL_ROWS, LANES), F32),
            cells,
            cells,
            cells,
            cells,
            pltpu.SemaphoreType.DMA((3,)),
            pltpu.SemaphoreType.DMA((4,)),
            pltpu.SemaphoreType.DMA((4,)),
            pltpu.SemaphoreType.DMA((7,)),
            pltpu.SemaphoreType.DMA((7,)),
            pltpu.SemaphoreType.DMA((4,)),
        ],
        compiler_params=pltpu.CompilerParams(
            collective_id=0, has_side_effects=True, vmem_limit_bytes=48 * 2**20
        ),
    )(pressure_source, geometry[0], owner, eigen, steps, tables)


def solution(mesh):
    eigen, steps, tables = eigen_table(), step_table(), transform_tables()

    def whole(pressure_source, geometry, owner):
        return jax.shard_map(
            on_device,
            mesh=mesh,
            in_specs=(P("span", "rows", None), P("span", None, "rows", None), P(), P(), P(), P()),
            out_specs=P("span", "rows", None),
            check_vma=False,
        )(pressure_source, geometry, owner, eigen, steps, tables)

    return whole
```

```python
import math

import jax
import jax.numpy as jnp
import ml_dtypes
import numpy as np
from jax import lax
from jax.experimental import pallas as pl
from jax.experimental.pallas import tpu as pltpu
from jax.sharding import PartitionSpec as P

MESH = pl.DeviceIdType.MESH
F32 = jnp.float32
BF16 = jnp.bfloat16

SWEEPS = 2
STEPS = 8
LOWER_BOUND = 0.02
UPPER_BOUND = 2.0
CENTER = (UPPER_BOUND + LOWER_BOUND) / 2.0
HALF_WIDTH = (UPPER_BOUND - LOWER_BOUND) / 2.0

NZ = 256
SPAN = 64
ROWS = 4
CELL_ROWS = NZ * 4
LANES = 128


def mode_numbers():
    slot = np.arange(NZ)
    return np.where(slot <= NZ // 2, slot, slot - NZ // 2), slot <= NZ // 2


def transform_tables():
    modes, is_real = mode_numbers()
    points = np.arange(NZ)
    angle = 2.0 * np.pi * ((modes[:, None] * points[None, :]) % NZ) / NZ
    forward = np.where(is_real[:, None], np.cos(angle), -np.sin(angle))
    weight = np.where((modes == 0) | (modes == NZ // 2), 1.0, 2.0)
    inverse = (forward * weight[:, None] / NZ).T
    pieces = []
    for table in (forward, inverse):
        high = table.astype(ml_dtypes.bfloat16)
        low = (table - high.astype(np.float64)).astype(ml_dtypes.bfloat16)
        pieces += [high, low]
    return np.stack(pieces)


def eigen_table():
    modes, _ = mode_numbers()
    return (2.0 - 2.0 * np.cos(2.0 * np.pi * modes / NZ)).astype(np.float32)


def step_table():
    sigma = CENTER / HALF_WIDTH
    keep, add = [], []
    for _ in range(SWEEPS):
        ratio = 1.0 / sigma
        for _ in range(STEPS):
            ratio_next = 1.0 / (2.0 * sigma - ratio)
            keep.append(ratio_next * ratio)
            add.append(2.0 * ratio_next / HALF_WIDTH)
            ratio = ratio_next
        keep[-1], add[-1] = 0.0, 1.0 / CENTER
    return np.array([keep, add], np.float32)


def transform(high, low, x):
    x_high = x.astype(BF16)
    x_low = (x - x_high.astype(F32)).astype(BF16)
    out = jnp.dot(high, x_high, preferred_element_type=F32)
    out += jnp.dot(high, x_low, preferred_element_type=F32)
    out += jnp.dot(low, x_high, preferred_element_type=F32)
    return out


def gathered(ref):
    return jnp.concatenate([ref[pl.ds(q, NZ, stride=4), :] for q in range(4)], axis=1)


def scattered(ref, value):
    for q in range(4):
        ref[pl.ds(q, NZ, stride=4), :] = value[:, q * LANES : (q + 1) * LANES]


def kernel(
    x_hbm,
    g_hbm,
    owner_ref,
    eigen_ref,
    step_ref,
    table_hbm,
    o_ref,
    x_ref,
    g_ref,
    table_ref,
    cells_out,
    cells_in,
    modes_out,
    plane_in,
    plane_out,
    modes_in,
    points_out,
    points_in,
    masked,
    part_x,
    sum_x,
    part_z,
    geo,
    coef,
    zed,
    acc,
    way_a,
    way_b,
    in_sem,
    send_sem,
    recv_sem,
    geo_send,
    geo_recv,
    self_sem,
):
    span = lax.axis_index("span")
    row = lax.axis_index("rows")
    zi = lax.rem(span, 8)
    xi = lax.rem(lax.div(span, 8), 4)
    yh = lax.div(span, 32)
    yl = lax.div(row, 2)
    core = lax.rem(row, 2)
    mine = span * 4 + row
    place = 64 * row + span

    def far_first(k, n):
        step = lax.div(k + 1, 2)
        return lax.rem(n // 2 + step + lax.rem(k, 2) * (n - 2 * step), n)

    def span_peer(d):
        zk, xk, yk = lax.rem(d, 8), lax.rem(lax.div(d, 8), 4), lax.div(d, 32)
        return (
            lax.rem(yh + 1 - yk, 2) * 32
            + lax.rem(xi + far_first(xk, 4), 4) * 8
            + lax.rem(zi + far_first(zk, 8), 8)
        )

    def any_peer(d):
        dc, dl = 1 - lax.rem(d, 2), 1 - lax.rem(lax.div(d, 2), 2)
        return span_peer(lax.div(d, 4)), lax.rem(yl + dl, 2) * 2 + lax.rem(core + dc, 2)

    def rows_of(ref, start, size, unit):
        return ref.at[pl.ds(pl.multiple_of(start, unit), size)]

    def push(src, dst, sems, peer):
        pltpu.make_async_remote_copy(
            src_ref=src,
            dst_ref=dst,
            send_sem=sems[0],
            recv_sem=sems[1],
            device_id=peer,
            device_id_type=MESH,
        ).start()

    def await_rows(ref, count, sem):
        pltpu.make_async_copy(ref.at[pl.ds(0, count)], ref.at[pl.ds(0, count)], sem).wait()

    fetch = [
        pltpu.make_async_copy(src, dst, in_sem.at[k])
        for k, (src, dst) in enumerate(
            ((x_hbm, x_ref), (g_hbm, g_ref), (table_hbm, table_ref))
        )
    ]
    for copy in fetch:
        copy.start()

    barrier = pltpu.get_barrier_semaphore()

    @pl.loop(0, SPAN - 1)
    def _(d):
        pl.semaphore_signal(barrier, inc=1, device_id=(span_peer(d), row), device_id_type=MESH)

    for d in range(1, ROWS):
        pl.semaphore_signal(
            barrier, inc=1, device_id=(span, lax.rem(row + d, ROWS)), device_id_type=MESH
        )

    fetch[1].wait()
    own = owner_ref[0] == span
    for x_to in range(4):
        for y_to in range(2):
            tile_row, half = divmod(y_to * 4 + x_to, 2)
            for z_to in range(8):
                for comp in range(3):
                    piece = g_ref[comp, 8 * tile_row + 4 * half : 8 * tile_row + 4 * half + 4,
                                  z_to * LANES : (z_to + 1) * LANES]
                    at = ((x_to * 2 + y_to) * 8 + z_to) * 12 + comp * 4
                    masked[at : at + 4, :] = jnp.where(own, piece, jnp.zeros_like(piece))

    fetch[0].wait()
    for to in range(SPAN):
        rows_at, cols_at = 4 * (to // 8), LANES * (to % 8)
        for j in range(4):
            cells_out[16 * to + 4 * j : 16 * to + 4 * j + 4, :] = x_ref[
                j, rows_at : rows_at + 4, cols_at : cols_at + LANES
            ]

    pl.semaphore_wait(barrier, SPAN - 1 + ROWS - 1)

    def geo_sems(k):
        return geo_send.at[k], geo_recv.at[k]

    def span_at(y, x, z):
        return y * 32 + x * 8 + z

    for d in range(1, 4):
        to = lax.rem(xi + d, 4)
        push(
            rows_of(masked, to * 192, 192, 8),
            rows_of(part_x, xi * 192, 192, 8),
            geo_sems(0),
            (span_at(yh, to, zi), row),
        )

    def sems(k):
        return send_sem.at[k], recv_sem.at[k]

    @pl.loop(0, SPAN - 1)
    def _(d):
        to = span_peer(d)
        push(
            rows_of(cells_out, to * 16, 16, 16),
            rows_of(cells_in, span * 16, 16, 16),
            sems(0),
            (to, row),
        )

    cells_in[pl.ds(pl.multiple_of(span * 16, 16), 16), :] = cells_out[
        pl.ds(pl.multiple_of(span * 16, 16), 16), :
    ]
    part_x[pl.ds(pl.multiple_of(xi * 192, 8), 192), :] = masked[
        pl.ds(pl.multiple_of(xi * 192, 8), 192), :
    ]

    await_rows(part_x, 576, geo_recv.at[0])
    sum_x[...] = part_x[0:192] + part_x[192:384] + part_x[384:576] + part_x[576:768]
    others = [(dy, dz) for dz in (4, 3, 5, 2, 6, 1, 7, 0) for dy in (1, 0)][:-1]
    others = [(lax.rem(yh + dy, 2), lax.rem(zi + dz, 8)) for dy, dz in others]
    part_here = 16 * (8 * yh + zi)
    for y_to, z_to in others:
        push(
            rows_of(sum_x, 12 * (8 * y_to + z_to), 12, 4),
            rows_of(part_z, part_here, 12, 4),
            geo_sems(1),
            (span_at(y_to, xi, z_to), row),
        )
    keep_z = pltpu.make_async_copy(
        rows_of(sum_x, 12 * (8 * yh + zi), 12, 4),
        rows_of(part_z, part_here, 12, 4),
        self_sem.at[0],
    )
    keep_z.start()
    await_rows(part_z, 180, geo_recv.at[1])
    keep_z.wait()
    total = part_z[0:12]
    for d in range(1, 16):
        total = total + part_z[16 * d : 16 * d + 12]
    sum_own = masked.at[pl.ds(768, 12)]
    masked[768:780, :] = total

    here = 12 * place
    for y_to, z_to in others:
        push(
            sum_own,
            rows_of(geo, here, 12, 4),
            geo_sems(2),
            (span_at(y_to, xi, z_to), row),
        )
    keep_geo = pltpu.make_async_copy(sum_own, rows_of(geo, here, 12, 4), self_sem.at[1])
    keep_geo.start()

    await_rows(cells_in, 1008, recv_sem.at[0])
    fetch[2].wait()
    scattered(modes_out, transform(table_ref[0], table_ref[1], gathered(cells_in)))

    def block(r, y, x):
        return rows_of(geo, 12 * (64 * r + 32 * y + 8 * x), 96, 8)

    await_rows(geo, 180, geo_recv.at[2])
    keep_geo.wait()
    for dx, dl in ((2, 1), (1, 1), (3, 1), (2, 0), (1, 0), (3, 0), (0, 1)):
        x_to, l_to = lax.rem(xi + dx, 4), lax.rem(yl + dl, 2)
        for y in range(2):
            push(
                block(row, y, xi),
                block(row, y, xi),
                (geo_send.at[3], geo_recv.at[4 + dx]),
                (span_at(yh, x_to, zi), 2 * l_to + core),
            )


    @pl.loop(0, NZ - 1)
    def _(d):
        to_span, to_row = any_peer(d)
        push(
            rows_of(modes_out, (to_span * 4 + to_row) * 4, 4, 4),
            rows_of(plane_in, place * 4, 4, 4),
            sems(1),
            (to_span, to_row),
        )

    keep_plane = pltpu.make_async_copy(
        rows_of(modes_out, mine * 4, 4, 4), rows_of(plane_in, place * 4, 4, 4), self_sem.at[2]
    )
    keep_plane.start()

    for dx, count in ((0, 192), (1, 384), (3, 384), (2, 384)):
        await_rows(geo, count, geo_recv.at[4 + dx])
        for l in range(2):
            for y in range(2):
                whole_block = block(2 * l + core, y, lax.rem(xi + 4 - dx, 4))
                push(
                    whole_block,
                    whole_block,
                    (geo_send.at[4], geo_recv.at[3]),
                    (span, 2 * yl + 1 - core),
                )
    await_rows(geo, 1536, geo_recv.at[3])

    await_rows(plane_in, 1020, recv_sem.at[1])
    keep_plane.wait()

    eigen = eigen_ref[mine]
    lane = lax.broadcasted_iota(jnp.int32, (8, LANES), 1)
    sub = lax.broadcasted_iota(jnp.int32, (8, LANES), 0)
    first_lane, last_lane = lane == 0, lane == LANES - 1
    first_sub, last_sub = sub == 0, sub == 7

    def face(comp, x, q, z):
        return geo[pl.ds(12 * (8 * x + z) + 4 * comp + q, 8, stride=384), :]

    def slot(i, z):
        return pl.ds((i * 8 + z) * 8, 8)

    def to_left(v):
        return pltpu.roll(v, LANES - 1, 1)

    def to_right(v):
        return pltpu.roll(v, 1, 1)

    for x in range(4):
        for q in range(4):
            i = 4 * x + q
            west = [face(0, x, q, z) for z in range(8)]
            moved = [to_left(w) for w in west] + [jnp.zeros((8, LANES), F32)]
            for z in range(8):
                north = face(1, x, q, z)
                if i < 15:
                    south = face(1, (i + 1) // 4, (i + 1) % 4, z)
                else:
                    south = jnp.where(last_sub, 0.0, pltpu.roll(face(1, 0, 0, z), 7, 0))
                east = jnp.where(last_lane, moved[z + 1], moved[z])
                inverse = 1.0 / (west[z] + east + north + south + eigen * face(2, x, q, z))
                west_in = jnp.where(first_lane, 0.0, west[z]) if z == 0 else west[z]
                north_in = jnp.where(first_sub, 0.0, north) if i == 0 else north
                coef[0, slot(i, z), :] = west_in * inverse
                coef[1, slot(i, z), :] = east * inverse
                coef[2, slot(i, z), :] = north_in * inverse
                coef[3, slot(i, z), :] = south * inverse
                value = plane_in[pl.ds(4 * (8 * x + z) + q, 8, stride=128), :] * inverse
                zed[slot(i, z), :] = value
                way_a[slot(i, z), :] = value * (1.0 / CENTER)
                acc[slot(i, z), :] = jnp.zeros((8, LANES), F32)

    lanes = lax.broadcasted_iota(jnp.int32, (64, LANES), 1)
    first_lanes, last_lanes = lanes == 0, lanes == LANES - 1

    def line(i):
        return pl.ds(64 * i, 64)

    def turned(v, shift):
        return jnp.concatenate(
            [pltpu.roll(v[8 * z : 8 * z + 8], shift, 0) for z in range(8)], axis=0
        )

    def residuals(ways, done):
        above, mid = turned(ways[line(15), :], 1), ways[line(0), :]
        for i in range(16):
            below = ways[line(i + 1), :] if i < 15 else turned(ways[line(0), :], 7)
            right, left = to_right(mid), to_left(mid)
            from_west = jnp.where(
                first_lanes, jnp.concatenate([right[56:], right[:56]], axis=0), right
            )
            from_east = jnp.where(
                last_lanes, jnp.concatenate([left[8:], left[:8]], axis=0), left
            )
            flow = coef[0, line(i), :] * from_west + coef[1, line(i), :] * from_east
            flow += coef[2, line(i), :] * above + coef[3, line(i), :] * below
            done(i, mid, zed[line(i), :] - mid + flow)
            above, mid = mid, below

    def two_steps(pair, carry):
        keep_a, add_a = step_ref[0, 2 * pair], step_ref[1, 2 * pair]
        keep_b, add_b = step_ref[0, 2 * pair + 1], step_ref[1, 2 * pair + 1]

        def first_done(i, mid, value):
            zed[line(i), :] = value
            way_b[line(i), :] = keep_a * mid + add_a * value

        def second_done(i, mid, value):
            zed[line(i), :] = value
            acc[line(i), :] += way_a[line(i), :] + mid
            way_a[line(i), :] = keep_b * mid + add_b * value

        residuals(way_a, first_done)
        residuals(way_b, second_done)
        return carry

    last = SWEEPS * STEPS - 2
    lax.fori_loop(0, last // 2, two_steps, 0)
    keep, add = step_ref[0, last], step_ref[1, last]

    def last_done(i, mid, value):
        total = acc[line(i), :] + mid + (keep * mid + add * value)
        x, q = divmod(i, 4)
        for z in range(8):
            plane_out[pl.ds(4 * (8 * x + z) + q, 8, stride=128), :] = total[8 * z : 8 * z + 8]

    residuals(way_a, last_done)

    @pl.loop(0, NZ - 1)
    def _(d):
        to_span, to_row = any_peer(d)
        push(
            rows_of(plane_out, (64 * to_row + to_span) * 4, 4, 4),
            rows_of(modes_in, mine * 4, 4, 4),
            sems(2),
            (to_span, to_row),
        )

    keep_modes = pltpu.make_async_copy(
        rows_of(plane_out, place * 4, 4, 4), rows_of(modes_in, mine * 4, 4, 4), self_sem.at[3]
    )
    keep_modes.start()
    await_rows(modes_in, 1020, recv_sem.at[2])
    keep_modes.wait()
    scattered(points_out, transform(table_ref[2], table_ref[3], gathered(modes_in)))

    @pl.loop(0, SPAN - 1)
    def _(d):
        to = span_peer(d)
        push(
            rows_of(points_out, to * 16, 16, 16),
            rows_of(points_in, span * 16, 16, 16),
            sems(3),
            (to, row),
        )

    points_in[pl.ds(pl.multiple_of(span * 16, 16), 16), :] = points_out[
        pl.ds(pl.multiple_of(span * 16, 16), 16), :
    ]
    await_rows(points_in, 1008, recv_sem.at[3])
    for source in range(SPAN):
        rows_at, cols_at = 4 * (source // 8), LANES * (source % 8)
        for j in range(4):
            o_ref[j, rows_at : rows_at + 4, cols_at : cols_at + LANES] = points_in[
                16 * source + 4 * j : 16 * source + 4 * j + 4, :
            ]

    await_rows(cells_out, 1008, send_sem.at[0])
    await_rows(modes_out, 1020, send_sem.at[1])
    await_rows(plane_out, 1020, send_sem.at[2])
    await_rows(points_out, 1008, send_sem.at[3])
    for k, count in enumerate((576, 180, 180, 1344, 1536)):
        await_rows(geo, count, geo_send.at[k])


def on_device(pressure_source, geometry, owner, eigen, steps, tables):
    vmem = pl.BlockSpec(memory_space=pltpu.VMEM)
    hbm = pl.BlockSpec(memory_space=pltpu.HBM)
    smem = pl.BlockSpec(memory_space=pltpu.SMEM)
    cells = pltpu.VMEM((CELL_ROWS, LANES), F32)
    return pl.pallas_call(
        kernel,
        out_shape=jax.ShapeDtypeStruct(pressure_source.shape, F32),
        in_specs=[hbm, hbm, smem, smem, smem, hbm],
        out_specs=vmem,
        scratch_shapes=[
            pltpu.VMEM(pressure_source.shape, F32),
            pltpu.VMEM(geometry.shape[1:], F32),
            pltpu.VMEM(tables.shape, BF16),
        ]
        + [cells] * 8
        + [
            pltpu.VMEM((784, LANES), F32),
            pltpu.VMEM((768, LANES), F32),
            pltpu.VMEM((192, LANES), F32),
            pltpu.VMEM((256, LANES), F32),
            pltpu.VMEM((3072, LANES), F32),
            pltpu.VMEM((4, CELL_ROWS, LANES), F32),
            cells,
            cells,
            cells,
            cells,
            pltpu.SemaphoreType.DMA((3,)),
            pltpu.SemaphoreType.DMA((4,)),
            pltpu.SemaphoreType.DMA((4,)),
            pltpu.SemaphoreType.DMA((5,)),
            pltpu.SemaphoreType.DMA((8,)),
            pltpu.SemaphoreType.DMA((4,)),
        ],
        compiler_params=pltpu.CompilerParams(
            collective_id=0, has_side_effects=True, vmem_limit_bytes=48 * 2**20
        ),
    )(pressure_source, geometry[0], owner, eigen, steps, tables)


def solution(mesh):
    eigen, steps, tables = eigen_table(), step_table(), transform_tables()

    def whole(pressure_source, geometry, owner):
        return jax.shard_map(
            on_device,
            mesh=mesh,
            in_specs=(P("span", "rows", None), P("span", None, "rows", None), P(), P(), P(), P()),
            out_specs=P("span", "rows", None),
            check_vma=False,
        )(pressure_source, geometry, owner, eigen, steps, tables)

    return whole
```

```python
import math

import jax
import jax.numpy as jnp
import ml_dtypes
import numpy as np
from jax import lax
from jax.experimental import pallas as pl
from jax.experimental.pallas import tpu as pltpu
from jax.sharding import PartitionSpec as P

MESH = pl.DeviceIdType.MESH
F32 = jnp.float32
BF16 = jnp.bfloat16

SWEEPS = 2
STEPS = 8
LOWER_BOUND = 0.02
UPPER_BOUND = 2.0
CENTER = (UPPER_BOUND + LOWER_BOUND) / 2.0
HALF_WIDTH = (UPPER_BOUND - LOWER_BOUND) / 2.0

NZ = 256
SPAN = 64
ROWS = 4
CELL_ROWS = NZ * 4
LANES = 128


def mode_numbers():
    slot = np.arange(NZ)
    return np.where(slot <= NZ // 2, slot, slot - NZ // 2), slot <= NZ // 2


def transform_tables():
    modes, is_real = mode_numbers()
    points = np.arange(NZ)
    angle = 2.0 * np.pi * ((modes[:, None] * points[None, :]) % NZ) / NZ
    forward = np.where(is_real[:, None], np.cos(angle), -np.sin(angle))
    weight = np.where((modes == 0) | (modes == NZ // 2), 1.0, 2.0)
    inverse = (forward * weight[:, None] / NZ).T
    pieces = []
    for table in (forward, inverse):
        high = table.astype(ml_dtypes.bfloat16)
        low = (table - high.astype(np.float64)).astype(ml_dtypes.bfloat16)
        pieces += [high, low]
    return np.stack(pieces)


def eigen_table():
    modes, _ = mode_numbers()
    return (2.0 - 2.0 * np.cos(2.0 * np.pi * modes / NZ)).astype(np.float32)


def step_table():
    sigma = CENTER / HALF_WIDTH
    keep, add = [], []
    for _ in range(SWEEPS):
        ratio = 1.0 / sigma
        for _ in range(STEPS):
            ratio_next = 1.0 / (2.0 * sigma - ratio)
            keep.append(ratio_next * ratio)
            add.append(2.0 * ratio_next / HALF_WIDTH)
            ratio = ratio_next
        keep[-1], add[-1] = 0.0, 1.0 / CENTER
    return np.array([keep, add], np.float32)


def transform(high, low, x):
    x_high = x.astype(BF16)
    x_low = (x - x_high.astype(F32)).astype(BF16)
    out = jnp.dot(high, x_high, preferred_element_type=F32)
    out += jnp.dot(high, x_low, preferred_element_type=F32)
    out += jnp.dot(low, x_high, preferred_element_type=F32)
    return out


def gathered(ref):
    return jnp.concatenate([ref[pl.ds(q, NZ, stride=4), :] for q in range(4)], axis=1)


def scattered(ref, value):
    for q in range(4):
        ref[pl.ds(q, NZ, stride=4), :] = value[:, q * LANES : (q + 1) * LANES]


def kernel(
    x_hbm,
    g_hbm,
    owner_ref,
    eigen_ref,
    step_ref,
    table_hbm,
    o_ref,
    x_ref,
    g_ref,
    table_ref,
    cells_out,
    cells_in,
    modes_out,
    plane_in,
    plane_out,
    modes_in,
    points_out,
    points_in,
    masked,
    part_x,
    sum_x,
    part_z,
    geo,
    coef,
    zed,
    acc,
    way_a,
    way_b,
    in_sem,
    send_sem,
    recv_sem,
    geo_send,
    geo_recv,
    self_sem,
):
    span = lax.axis_index("span")
    row = lax.axis_index("rows")
    zi = lax.rem(span, 8)
    xi = lax.rem(lax.div(span, 8), 4)
    yh = lax.div(span, 32)
    yl = lax.div(row, 2)
    core = lax.rem(row, 2)
    mine = span * 4 + row
    place = 64 * row + span

    def far_first(k, n):
        step = lax.div(k + 1, 2)
        return lax.rem(n // 2 + step + lax.rem(k, 2) * (n - 2 * step), n)

    def span_peer(d):
        zk, xk, yk = lax.rem(d, 8), lax.rem(lax.div(d, 8), 4), lax.div(d, 32)
        return (
            lax.rem(yh + 1 - yk, 2) * 32
            + lax.rem(xi + far_first(xk, 4), 4) * 8
            + lax.rem(zi + far_first(zk, 8), 8)
        )

    def any_peer(d):
        dc, dl = 1 - lax.rem(d, 2), 1 - lax.rem(lax.div(d, 2), 2)
        return span_peer(lax.div(d, 4)), lax.rem(yl + dl, 2) * 2 + lax.rem(core + dc, 2)

    def rows_of(ref, start, size, unit):
        return ref.at[pl.ds(pl.multiple_of(start, unit), size)]

    def push(src, dst, sems, peer):
        pltpu.make_async_remote_copy(
            src_ref=src,
            dst_ref=dst,
            send_sem=sems[0],
            recv_sem=sems[1],
            device_id=peer,
            device_id_type=MESH,
        ).start()

    def await_rows(ref, count, sem):
        pltpu.make_async_copy(ref.at[pl.ds(0, count)], ref.at[pl.ds(0, count)], sem).wait()

    fetch = [
        pltpu.make_async_copy(src, dst, in_sem.at[k])
        for k, (src, dst) in enumerate(
            ((x_hbm, x_ref), (g_hbm, g_ref), (table_hbm, table_ref))
        )
    ]
    for copy in fetch:
        copy.start()

    barrier = pltpu.get_barrier_semaphore()

    @pl.loop(0, SPAN - 1)
    def _(d):
        pl.semaphore_signal(barrier, inc=1, device_id=(span_peer(d), row), device_id_type=MESH)

    for d in range(1, ROWS):
        pl.semaphore_signal(
            barrier, inc=1, device_id=(span, lax.rem(row + d, ROWS)), device_id_type=MESH
        )

    fetch[1].wait()
    own = owner_ref[0] == span
    for x_to in range(4):
        for y_to in range(2):
            tile_row, half = divmod(y_to * 4 + x_to, 2)
            for z_to in range(8):
                for comp in range(3):
                    piece = g_ref[comp, 8 * tile_row + 4 * half : 8 * tile_row + 4 * half + 4,
                                  z_to * LANES : (z_to + 1) * LANES]
                    at = ((x_to * 2 + y_to) * 8 + z_to) * 12 + comp * 4
                    masked[at : at + 4, :] = jnp.where(own, piece, jnp.zeros_like(piece))

    fetch[0].wait()
    for to in range(SPAN):
        rows_at, cols_at = 4 * (to // 8), LANES * (to % 8)
        for j in range(4):
            cells_out[16 * to + 4 * j : 16 * to + 4 * j + 4, :] = x_ref[
                j, rows_at : rows_at + 4, cols_at : cols_at + LANES
            ]

    pl.semaphore_wait(barrier, SPAN - 1 + ROWS - 1)

    def geo_sems(k):
        return geo_send.at[k], geo_recv.at[k]

    def span_at(y, x, z):
        return y * 32 + x * 8 + z

    for d in range(1, 4):
        to = lax.rem(xi + d, 4)
        push(
            rows_of(masked, to * 192, 192, 8),
            rows_of(part_x, xi * 192, 192, 8),
            geo_sems(0),
            (span_at(yh, to, zi), row),
        )

    def sems(k):
        return send_sem.at[k], recv_sem.at[k]

    @pl.loop(0, SPAN - 1)
    def _(d):
        to = span_peer(d)
        push(
            rows_of(cells_out, to * 16, 16, 16),
            rows_of(cells_in, span * 16, 16, 16),
            sems(0),
            (to, row),
        )

    cells_in[pl.ds(pl.multiple_of(span * 16, 16), 16), :] = cells_out[
        pl.ds(pl.multiple_of(span * 16, 16), 16), :
    ]
    part_x[pl.ds(pl.multiple_of(xi * 192, 8), 192), :] = masked[
        pl.ds(pl.multiple_of(xi * 192, 8), 192), :
    ]

    await_rows(part_x, 576, geo_recv.at[0])
    sum_x[...] = part_x[0:192] + part_x[192:384] + part_x[384:576] + part_x[576:768]
    others = [(dy, dz) for dz in (4, 3, 5, 2, 6, 1, 7, 0) for dy in (1, 0)][:-1]
    others = [(lax.rem(yh + dy, 2), lax.rem(zi + dz, 8)) for dy, dz in others]
    part_here = 16 * (8 * yh + zi)
    for y_to, z_to in others:
        push(
            rows_of(sum_x, 12 * (8 * y_to + z_to), 12, 4),
            rows_of(part_z, part_here, 12, 4),
            geo_sems(1),
            (span_at(y_to, xi, z_to), row),
        )
    keep_z = pltpu.make_async_copy(
        rows_of(sum_x, 12 * (8 * yh + zi), 12, 4),
        rows_of(part_z, part_here, 12, 4),
        self_sem.at[0],
    )
    keep_z.start()
    await_rows(part_z, 180, geo_recv.at[1])
    keep_z.wait()
    total = part_z[0:12]
    for d in range(1, 16):
        total = total + part_z[16 * d : 16 * d + 12]
    sum_own = masked.at[pl.ds(768, 12)]
    masked[768:780, :] = total

    here = 12 * place
    for y_to, z_to in others:
        push(
            sum_own,
            rows_of(geo, here, 12, 4),
            geo_sems(2),
            (span_at(y_to, xi, z_to), row),
        )
    keep_geo = pltpu.make_async_copy(sum_own, rows_of(geo, here, 12, 4), self_sem.at[1])
    keep_geo.start()

    await_rows(cells_in, 1008, recv_sem.at[0])
    fetch[2].wait()
    scattered(modes_out, transform(table_ref[0], table_ref[1], gathered(cells_in)))

    def block(r, y, x):
        return rows_of(geo, 12 * (64 * r + 32 * y + 8 * x), 96, 8)

    await_rows(geo, 180, geo_recv.at[2])
    keep_geo.wait()
    for dx, dl in ((2, 1), (1, 1), (3, 1), (2, 0), (1, 0), (3, 0), (0, 1)):
        x_to, l_to = lax.rem(xi + dx, 4), lax.rem(yl + dl, 2)
        for y in range(2):
            push(
                block(row, y, xi),
                block(row, y, xi),
                (geo_send.at[3], geo_recv.at[4 + dx]),
                (span_at(yh, x_to, zi), 2 * l_to + core),
            )


    @pl.loop(0, NZ - 1)
    def _(d):
        to_span, to_row = any_peer(d)
        push(
            rows_of(modes_out, (to_span * 4 + to_row) * 4, 4, 4),
            rows_of(plane_in, place * 4, 4, 4),
            sems(1),
            (to_span, to_row),
        )

    keep_plane = pltpu.make_async_copy(
        rows_of(modes_out, mine * 4, 4, 4), rows_of(plane_in, place * 4, 4, 4), self_sem.at[2]
    )
    keep_plane.start()

    for dx, count in ((0, 192), (1, 384), (3, 384), (2, 384)):
        await_rows(geo, count, geo_recv.at[4 + dx])
        for l in range(2):
            for y in range(2):
                whole_block = block(2 * l + core, y, lax.rem(xi + 4 - dx, 4))
                push(
                    whole_block,
                    whole_block,
                    (geo_send.at[4], geo_recv.at[3]),
                    (span, 2 * yl + 1 - core),
                )
    await_rows(geo, 1536, geo_recv.at[3])


    eigen = eigen_ref[mine]
    lane = lax.broadcasted_iota(jnp.int32, (8, LANES), 1)
    sub = lax.broadcasted_iota(jnp.int32, (8, LANES), 0)
    first_lane, last_lane = lane == 0, lane == LANES - 1
    first_sub, last_sub = sub == 0, sub == 7

    def face(comp, x, q, z):
        return geo[pl.ds(12 * (8 * x + z) + 4 * comp + q, 8, stride=384), :]

    def slot(i, z):
        return pl.ds((i * 8 + z) * 8, 8)

    def to_left(v):
        return pltpu.roll(v, LANES - 1, 1)

    def to_right(v):
        return pltpu.roll(v, 1, 1)

    for x in range(4):
        for q in range(4):
            i = 4 * x + q
            west = [face(0, x, q, z) for z in range(8)]
            moved = [to_left(w) for w in west] + [jnp.zeros((8, LANES), F32)]
            for z in range(8):
                north = face(1, x, q, z)
                if i < 15:
                    south = face(1, (i + 1) // 4, (i + 1) % 4, z)
                else:
                    south = jnp.where(last_sub, 0.0, pltpu.roll(face(1, 0, 0, z), 7, 0))
                east = jnp.where(last_lane, moved[z + 1], moved[z])
                inverse = 1.0 / (west[z] + east + north + south + eigen * face(2, x, q, z))
                west_in = jnp.where(first_lane, 0.0, west[z]) if z == 0 else west[z]
                north_in = jnp.where(first_sub, 0.0, north) if i == 0 else north
                coef[0, slot(i, z), :] = west_in * inverse
                coef[1, slot(i, z), :] = east * inverse
                coef[2, slot(i, z), :] = north_in * inverse
                coef[3, slot(i, z), :] = south * inverse
                way_b[slot(i, z), :] = inverse

    await_rows(plane_in, 1020, recv_sem.at[1])
    keep_plane.wait()
    for x in range(4):
        for q in range(4):
            i = 4 * x + q
            for z in range(8):
                value = plane_in[pl.ds(4 * (8 * x + z) + q, 8, stride=128), :]
                value = value * way_b[slot(i, z), :]
                zed[slot(i, z), :] = value
                way_a[slot(i, z), :] = value * (1.0 / CENTER)
                acc[slot(i, z), :] = jnp.zeros((8, LANES), F32)

    lanes = lax.broadcasted_iota(jnp.int32, (64, LANES), 1)
    first_lanes, last_lanes = lanes == 0, lanes == LANES - 1

    def line(i):
        return pl.ds(64 * i, 64)

    def turned(v, shift):
        return jnp.concatenate(
            [pltpu.roll(v[8 * z : 8 * z + 8], shift, 0) for z in range(8)], axis=0
        )

    def residuals(ways, done):
        above, mid = turned(ways[line(15), :], 1), ways[line(0), :]
        for i in range(16):
            below = ways[line(i + 1), :] if i < 15 else turned(ways[line(0), :], 7)
            right, left = to_right(mid), to_left(mid)
            from_west = jnp.where(
                first_lanes, jnp.concatenate([right[56:], right[:56]], axis=0), right
            )
            from_east = jnp.where(
                last_lanes, jnp.concatenate([left[8:], left[:8]], axis=0), left
            )
            flow = coef[0, line(i), :] * from_west + coef[1, line(i), :] * from_east
            flow += coef[2, line(i), :] * above + coef[3, line(i), :] * below
            done(i, mid, zed[line(i), :] - mid + flow)
            above, mid = mid, below

    def two_steps(pair, carry):
        keep_a, add_a = step_ref[0, 2 * pair], step_ref[1, 2 * pair]
        keep_b, add_b = step_ref[0, 2 * pair + 1], step_ref[1, 2 * pair + 1]

        def first_done(i, mid, value):
            zed[line(i), :] = value
            way_b[line(i), :] = keep_a * mid + add_a * value

        def second_done(i, mid, value):
            zed[line(i), :] = value
            acc[line(i), :] += way_a[line(i), :] + mid
            way_a[line(i), :] = keep_b * mid + add_b * value

        residuals(way_a, first_done)
        residuals(way_b, second_done)
        return carry

    last = SWEEPS * STEPS - 2
    lax.fori_loop(0, last // 2, two_steps, 0)
    keep, add = step_ref[0, last], step_ref[1, last]

    def last_done(i, mid, value):
        total = acc[line(i), :] + mid + (keep * mid + add * value)
        x, q = divmod(i, 4)
        for z in range(8):
            plane_out[pl.ds(4 * (8 * x + z) + q, 8, stride=128), :] = total[8 * z : 8 * z + 8]

    residuals(way_a, last_done)

    @pl.loop(0, NZ - 1)
    def _(d):
        to_span, to_row = any_peer(d)
        push(
            rows_of(plane_out, (64 * to_row + to_span) * 4, 4, 4),
            rows_of(modes_in, mine * 4, 4, 4),
            sems(2),
            (to_span, to_row),
        )

    keep_modes = pltpu.make_async_copy(
        rows_of(plane_out, place * 4, 4, 4), rows_of(modes_in, mine * 4, 4, 4), self_sem.at[3]
    )
    keep_modes.start()
    await_rows(modes_in, 1020, recv_sem.at[2])
    keep_modes.wait()
    scattered(points_out, transform(table_ref[2], table_ref[3], gathered(modes_in)))

    @pl.loop(0, SPAN - 1)
    def _(d):
        to = span_peer(d)
        push(
            rows_of(points_out, to * 16, 16, 16),
            rows_of(points_in, span * 16, 16, 16),
            sems(3),
            (to, row),
        )

    points_in[pl.ds(pl.multiple_of(span * 16, 16), 16), :] = points_out[
        pl.ds(pl.multiple_of(span * 16, 16), 16), :
    ]
    await_rows(points_in, 1008, recv_sem.at[3])
    for source in range(SPAN):
        rows_at, cols_at = 4 * (source // 8), LANES * (source % 8)
        for j in range(4):
            o_ref[j, rows_at : rows_at + 4, cols_at : cols_at + LANES] = points_in[
                16 * source + 4 * j : 16 * source + 4 * j + 4, :
            ]

    await_rows(cells_out, 1008, send_sem.at[0])
    await_rows(modes_out, 1020, send_sem.at[1])
    await_rows(plane_out, 1020, send_sem.at[2])
    await_rows(points_out, 1008, send_sem.at[3])
    for k, count in enumerate((576, 180, 180, 1344, 1536)):
        await_rows(geo, count, geo_send.at[k])


def on_device(pressure_source, geometry, owner, eigen, steps, tables):
    vmem = pl.BlockSpec(memory_space=pltpu.VMEM)
    hbm = pl.BlockSpec(memory_space=pltpu.HBM)
    smem = pl.BlockSpec(memory_space=pltpu.SMEM)
    cells = pltpu.VMEM((CELL_ROWS, LANES), F32)
    return pl.pallas_call(
        kernel,
        out_shape=jax.ShapeDtypeStruct(pressure_source.shape, F32),
        in_specs=[hbm, hbm, smem, smem, smem, hbm],
        out_specs=vmem,
        scratch_shapes=[
            pltpu.VMEM(pressure_source.shape, F32),
            pltpu.VMEM(geometry.shape[1:], F32),
            pltpu.VMEM(tables.shape, BF16),
        ]
        + [cells] * 8
        + [
            pltpu.VMEM((784, LANES), F32),
            pltpu.VMEM((768, LANES), F32),
            pltpu.VMEM((192, LANES), F32),
            pltpu.VMEM((256, LANES), F32),
            pltpu.VMEM((3072, LANES), F32),
            pltpu.VMEM((4, CELL_ROWS, LANES), F32),
            cells,
            cells,
            cells,
            cells,
            pltpu.SemaphoreType.DMA((3,)),
            pltpu.SemaphoreType.DMA((4,)),
            pltpu.SemaphoreType.DMA((4,)),
            pltpu.SemaphoreType.DMA((5,)),
            pltpu.SemaphoreType.DMA((8,)),
            pltpu.SemaphoreType.DMA((4,)),
        ],
        compiler_params=pltpu.CompilerParams(
            collective_id=0, has_side_effects=True, vmem_limit_bytes=48 * 2**20
        ),
    )(pressure_source, geometry[0], owner, eigen, steps, tables)


def solution(mesh):
    eigen, steps, tables = eigen_table(), step_table(), transform_tables()

    def whole(pressure_source, geometry, owner):
        return jax.shard_map(
            on_device,
            mesh=mesh,
            in_specs=(P("span", "rows", None), P("span", None, "rows", None), P(), P(), P(), P()),
            out_specs=P("span", "rows", None),
            check_vma=False,
        )(pressure_source, geometry, owner, eigen, steps, tables)

    return whole
```
